32 devices in a mesh: rows: 8 (over y, x, core), cols: 4 (over z).
Axes of the slice: x: 2, y: 2, z: 4, core: 2. Of those that a mesh axis runs over, the one named last changes fastest.
Arguments:
- coords: int32 [8, 16384], P(None, ('rows', 'cols')), may hold values from 0 to 4095
- probes: float32 [64, 16384], P(None, ('rows', 'cols')), may hold values from -6 to 6
- lengthscales: float32 [8], replicated, may hold values from 0.15 to 0.25
- amplitude: float32 [1], replicated, may hold values from 0.1 to 0.3
- landmarks: float32 [14, 8, 128], replicated, may hold values from 0 to 1
- coupling: float32 [128, 128], replicated, may hold values from -0.5 to 0.5
Outputs:
- products: float32 [2, 64, 16384], P(None, None, ('rows', 'cols'))
The draws below stay inside these ranges and needn't reach their ends.
All inputs are finite; a program needn't handle non-finite values.
Results may differ from the reference program's by a relative error of at most 0.0025.
Values may be sent and summed in bfloat16 or wider, within the bound.
A program may use at most 64 MiB of HBM per device.

```python
import math
import jax
import jax.numpy as jnp
from jax import lax

DIMS = 8
RANK = 128
PROBES = 64
LEAF = 2048
POINTS = 16384
LEVELS = 3
N_ROWS = 8


def radius_at(depth):
    return max(32, 768 >> depth - 1)


def tree_centres(key):
    centres = jnp.full((DIMS, 1), 2048, jnp.int32)
    listing = []
    for depth in range(1, LEVELS + 1):
        radius = radius_at(depth)
        count = 1 << depth
        offsets = jax.random.randint(jax.random.fold_in(key, 1000 + depth), (DIMS, count), -radius, radius + 1, jnp.int32)
        centres = jnp.repeat(centres, 2, axis=1) + offsets
        listing.append(centres)
    return listing


def draw_coords(key, part):
    leaf_centres = tree_centres(key)[-1]
    spread = jax.random.randint(jax.random.fold_in(key, 77), (DIMS, POINTS), -1024, 1025, jnp.int32)
    placed = jnp.clip(jnp.repeat(leaf_centres, LEAF, axis=1) + spread, 0, 4095)
    chosen = jax.random.randint(jax.random.fold_in(key, 78), (2,), 0, POINTS, jnp.int32)
    placed = placed.at[0, chosen[0]].set(4095)
    placed = placed.at[1, chosen[1]].set(0)
    return placed


def draw_landmarks(key, part):
    listing = tree_centres(key)
    blocks = []
    for depth in range(1, LEVELS + 1):
        deeper = sum((radius_at(lower) * radius_at(lower) for lower in range(depth + 1, LEVELS + 1)))
        half_width = math.sqrt(deeper + 1048576.0)
        count = 1 << depth
        centres = listing[depth - 1].astype(jnp.float32)
        jitter = jax.random.uniform(jax.random.fold_in(key, 2000 + depth), (count, DIMS, RANK), jnp.float32, -1.0, 1.0)
        placed = (jnp.transpose(centres)[:, :, None] + half_width * jitter) / 4096.0
        blocks.append(jnp.clip(placed, 0.0, 1.0))
    return jnp.concatenate(blocks, axis=0)


def block_levels(key, dims, cuts, low, high):
    factor_of = 1.0
    for axis_at, blocks in cuts:
        draws = jax.random.uniform(jax.random.fold_in(jax.random.fold_in(key, 6), axis_at), (blocks,), jnp.float32, low / len(cuts), high / len(cuts))
        factor_of = factor_of * jnp.repeat(jnp.exp(draws), dims[axis_at] // blocks).reshape((-1,) + (1,) * (len(dims) - 1 - axis_at))
    return factor_of


def normal_values(stream_key, dims, scale, most, pieces=(), held_as=jnp.bfloat16):
    array = jax.random.normal(stream_key, dims, jnp.float32) * scale
    if len(pieces) > 0:
        array = block_levels(stream_key, dims, pieces, -0.22, 0.18) * array
    return jnp.clip(array, min=-most, max=most).astype(held_as)


def setup_inputs(seed: int = 0) -> dict:
    seeds = jax.random.split(jax.random.key(seed), 7)
    coords = draw_coords(jax.random.fold_in(seeds[6], 71), 0)
    probes = normal_values(seeds[1], (PROBES, POINTS), 1.0, 6.0, ((1, 32),), jnp.float32)
    lengthscales = jnp.clip(jnp.exp(jax.random.uniform(seeds[2], (DIMS,), jnp.float32, math.log(0.15), math.log(0.25))), 0.15, 0.25)
    amplitude = jnp.clip(jnp.exp(jax.random.uniform(seeds[3], (1,), jnp.float32, math.log(0.1), math.log(0.3))), 0.1, 0.3)
    landmarks = draw_landmarks(jax.random.fold_in(seeds[6], 71), 0)
    coupling = normal_values(seeds[5], (RANK, RANK), RANK ** -0.5, 0.5, (), jnp.float32)
    return {"coords": coords, "probes": probes, "lengthscales": lengthscales, "amplitude": amplitude, "landmarks": landmarks, "coupling": coupling}


def pair_squares(left_points, right_points):
    squared = jnp.zeros((left_points.shape[1], right_points.shape[1]), jnp.float32)
    for component in range(left_points.shape[0]):
        offset = left_points[component][:, None] - right_points[component][None, :]
        squared = squared + offset * offset
    return squared


def reference(coords, probes, lengthscales, amplitude, landmarks, coupling):
    highest = lax.Precision.HIGHEST
    inverse_scale = 1.0 / lengthscales
    scaled = coords.astype(jnp.float32) * (1.0 / 4096.0) * inverse_scale[:, None]
    anchors = landmarks * inverse_scale[None, :, None]
    strength = amplitude[0]
    signs = probes
    signs_half = signs.astype(jnp.bfloat16)

    leaf_points = jnp.transpose(scaled.reshape(DIMS, N_ROWS, LEAF), (1, 0, 2))
    leaf_signs = jnp.transpose(signs_half.reshape(PROBES, N_ROWS, LEAF), (1, 0, 2))

    def leaf_block(items):
        points, sign_rows = items
        squared = pair_squares(points, points)
        kernel = strength * jnp.exp(-0.5 * squared)
        kernel_half = kernel.astype(jnp.bfloat16)
        slope_half = (kernel * squared).astype(jnp.bfloat16)
        return jnp.stack([jnp.dot(sign_rows, kernel_half, preferred_element_type=jnp.float32),
                          jnp.dot(sign_rows, slope_half, preferred_element_type=jnp.float32)])

    diagonal = lax.map(leaf_block, (leaf_points, leaf_signs))
    result = jnp.transpose(diagonal, (1, 2, 0, 3)).reshape(2, PROBES, POINTS)

    cores = jnp.stack([coupling.T, coupling])
    for depth in range(1, LEVELS + 1):
        count = 2 ** depth
        members = POINTS // count
        node_points = scaled.reshape(DIMS, count, members)
        node_anchors = anchors[count - 2:2 * count - 2]
        squared = jnp.zeros((count, members, RANK), jnp.float32)
        for component in range(DIMS):
            offset = node_points[component][:, :, None] - node_anchors[:, component, None, :]
            squared = squared + offset * offset
        factor = strength * jnp.exp(-0.5 * squared)
        dfactor = factor * squared
        node_signs = signs.reshape(PROBES, count, members)
        project = jnp.einsum('pnm,nmr->npr', node_signs, factor, precision=highest)
        dproject = jnp.einsum('pnm,nmr->npr', node_signs, dfactor, precision=highest)
        sib_project = project.reshape(count // 2, 2, PROBES, RANK)[:, ::-1].reshape(count, PROBES, RANK)
        sib_dproject = dproject.reshape(count // 2, 2, PROBES, RANK)[:, ::-1].reshape(count, PROBES, RANK)
        node_cores = jnp.tile(cores, (count // 2, 1, 1))
        first = jnp.einsum('npr,nrs->nps', sib_project, node_cores, precision=highest)
        second = jnp.einsum('npr,nrs->nps', sib_dproject, node_cores, precision=highest)
        value = jnp.einsum('nps,nms->pnm', first, factor, precision=highest)
        slope = jnp.einsum('nps,nms->pnm', first, dfactor, precision=highest) + jnp.einsum('nps,nms->pnm', second, factor, precision=highest)
        result = result + jnp.stack([value.reshape(PROBES, POINTS), slope.reshape(PROBES, POINTS)])
    return result
```

```python
import functools
import math

import jax
import jax.numpy as jnp
from jax import lax
from jax.experimental import pallas as pl
from jax.experimental.pallas import tpu as pltpu
from jax.sharding import PartitionSpec as P

F32 = jnp.float32
BF16 = jnp.bfloat16
HALF_LOG2E = 0.5 / math.log(2.0)
UNIT = HALF_LOG2E / 4096.0**2
MESH = pl.DeviceIdType.MESH
LANES = 128


def toggled(index, mask):
    bit = 1
    while bit <= mask:
        if mask & bit:
            index = index + bit - 2 * bit * ((index // bit) % 2)
        bit *= 2
    return index


def halves(x):
    high = x.astype(BF16)
    return high, (x - high.astype(F32)).astype(BF16)


def thirds(x):
    first = x.astype(BF16).astype(F32)
    rest = x - first
    second = rest.astype(BF16).astype(F32)
    return first, second, rest - second


def rows_of(pieces, shape):
    at = lax.broadcasted_iota(jnp.int32, shape, 0)
    out = jnp.zeros(shape, F32)
    for i, piece in enumerate(pieces):
        out = jnp.where(at == i, piece, out)
    return out


def padded(groups):
    n = groups[0].shape[1]
    rest = LANES - sum(g.shape[0] for g in groups)
    return jnp.concatenate(groups + [jnp.zeros((rest, n), F32)], axis=0)


def dot(a, b):
    return jnp.dot(a, b, preferred_element_type=F32)


def dot_t(a, b):
    return lax.dot_general(a, b, (((1,), (1,)), ((), ())), preferred_element_type=F32)


def kernel(
    groups, levels,
    scale_ref, amp_ref, coords_ref, probes_ref, land_ref, coup_ref, out_ref,
    half, cbuf, pbuf, lhs, fac, grown, proj, send_a, recv_a, send_b, recv_b,
    gs_sem, gr_sem, as_sem, ar_sem, bs_sem, br_sem,
):
    row, col = lax.axis_index("rows"), lax.axis_index("cols")
    width = coords_ref.shape[1]
    probes = probes_ref.shape[0]
    rank = coup_ref.shape[0]

    targets = []
    for level in range(1, levels):
        for m in range(2 ** (level - 1)):
            targets.append((level, (1 << level) ^ (2 * m)))
    peers = [(row, toggled(col, k)) for k in range(1, groups)]
    peers.append((toggled(row, 1), col))
    peers += [(toggled(row, mask), col) for _, mask in targets]

    barrier = pltpu.get_barrier_semaphore()
    for peer in peers:
        pl.semaphore_signal(barrier, inc=1, device_id=peer, device_id_type=MESH)
    half[...] = probes_ref[...].astype(BF16)
    pl.semaphore_wait(barrier, len(peers))

    gathers = []
    for k in range(1, groups):
        peer = (row, toggled(col, k))
        pair = [
            pltpu.make_async_remote_copy(
                src_ref=src, dst_ref=dst.at[k - 1], send_sem=gs_sem.at[k - 1, i], recv_sem=gr_sem.at[k - 1, i],
                device_id=peer, device_id_type=MESH,
            )
            for i, (src, dst) in enumerate(((coords_ref, cbuf), (half, pbuf)))
        ]
        for copy in pair:
            copy.start()
        gathers.append(pair)

    at = lax.broadcasted_iota(jnp.int32, (8, LANES), 0)
    scales = jnp.ones((8, LANES), F32)
    for d in range(8):
        scales = jnp.where(at == d, scale_ref[d], scales)
    weight = (1.0 / (scales * scales))[:, :1] * UNIT
    log_amp = jnp.log(jnp.full((1, LANES), amp_ref[0], F32)) * (1.0 / math.log(2.0))
    log_amp = log_amp[:, :1]
    offset = log_amp * (1.0 / HALF_LOG2E)
    slant = 1.0 / HALF_LOG2E

    def centred(coords):
        return (coords - 2048).astype(F32)

    own = centred(coords_ref[...])
    anchors = []
    for level in range(levels):
        depth = levels - level
        chosen = land_ref[2**depth - 2 + row // (1 << level)]
        anchors.append((chosen - 0.5) * 4096.0)
    left = jnp.concatenate([own] + anchors, axis=1)
    weighted = weight * left
    y1, y2, y3 = thirds(2.0 * weighted)
    norm = log_amp - jnp.sum(weighted * left, axis=0, keepdims=True)
    ones = jnp.ones_like(norm)
    special = rows_of(list(thirds(norm)) + [ones] * 3, left.shape)
    lhs[...] = jnp.transpose(padded([y1, y1, y2, y2, y3, y3, special])).astype(BF16)

    def features(coords):
        value = centred(coords)
        high = value.astype(BF16).astype(F32)
        low = value - high
        norm = -jnp.sum(weight * value * value, axis=0, keepdims=True)
        ones = jnp.ones_like(norm)
        special = rows_of([ones] * 3 + list(thirds(norm)), value.shape)
        return padded([high, low, high, low, high, low, special]).astype(BF16)

    def pair_of(start, feat):
        power = dot(lhs[start : start + LANES, :], feat)
        kern = jnp.exp2(power)
        return kern, kern * (offset - slant * power)

    def diagonal(feat, signs, first):
        for j in range(0, width, LANES):
            kern, slope = pair_of(j, feat)
            both = jnp.concatenate([kern.astype(BF16), slope.astype(BF16)], axis=0)
            got = dot_t(signs, both)
            for i in range(2):
                part = got[:, i * LANES : (i + 1) * LANES]
                if first:
                    out_ref[i, :, j : j + LANES] = part
                else:
                    out_ref[i, :, j : j + LANES] += part

    def project(feat, signs, first):
        for level in range(levels):
            kern, slope = pair_of(width + level * rank, feat)
            pieces = halves(kern) + halves(slope)
            if first:
                for i in range(4):
                    fac[i, level] = pieces[i]
            got = dot_t(signs, jnp.concatenate(pieces, axis=0))
            for i in range(2):
                part = got[:, 2 * i * rank : (2 * i + 1) * rank] + got[:, (2 * i + 1) * rank : (2 * i + 2) * rank]
                if first:
                    proj[level, i] = part
                else:
                    proj[level, i] += part

    feat = features(coords_ref[...])
    project(feat, half[...], True)
    diagonal(feat, half[...], True)

    coupling = coup_ref[...]
    flipped = jnp.transpose(coupling)
    for level in range(levels):
        side = ((row // (1 << level)) % 2).astype(F32)
        core = jnp.where(jnp.full((rank, rank), side) < 0.5, flipped, coupling)
        high, low = halves(core)
        both = jnp.concatenate([high, low], axis=0)
        for i in range(2):
            got = dot(both, fac[2 * i, level])
            total = got[:rank] + got[rank:] + dot(high, fac[2 * i + 1, level])
            g_high, g_low = halves(total)
            grown[2 * i, level * rank : (level + 1) * rank, :] = g_high
            grown[2 * i + 1, level * rank : (level + 1) * rank, :] = g_low

    for k in range(1, groups):
        for copy in gathers[k - 1]:
            copy.wait_recv()
        feat = features(cbuf[k - 1])
        signs = pbuf[k - 1]
        project(feat, signs, False)
        if k < groups - 1:
            diagonal(feat, signs, False)

    send_a[...] = proj[...].astype(send_a.dtype)
    swap = pltpu.make_async_remote_copy(
        src_ref=send_a, dst_ref=recv_a, send_sem=as_sem, recv_sem=ar_sem,
        device_id=(toggled(row, 1), col), device_id_type=MESH,
    )
    swap.start()
    if groups > 1:
        diagonal(feat, signs, False)
    swap.wait_recv()

    send_b[...] = (proj[1:] + recv_a[1:].astype(F32)).astype(send_b.dtype)
    hops = []
    for i, (level, mask) in enumerate(targets):
        copy = pltpu.make_async_remote_copy(
            src_ref=send_b.at[level - 1], dst_ref=recv_b.at[i], send_sem=bs_sem.at[i], recv_sem=br_sem.at[i],
            device_id=(toggled(row, mask), col), device_id_type=MESH,
        )
        copy.start()
        hops.append(copy)

    def apply(sums, low_row, high_row):
        high, low = halves(sums)
        both = jnp.concatenate([high, low], axis=0)
        g = [grown[i, low_row:high_row, :] for i in range(4)]
        a = dot(both, g[0])
        b = dot(high, g[1])
        c = dot(jnp.concatenate([high[:probes], low[:probes]], axis=0), g[2])
        d = dot(high[:probes], g[3])
        plain = a[: 2 * probes] + a[2 * probes :] + b
        out_ref[0] += plain[:probes]
        out_ref[1] += plain[probes:] + c[:probes] + c[probes:] + d

    apply(jnp.concatenate([recv_a[0, 0], recv_a[0, 1]], axis=0).astype(F32), 0, rank)
    for copy in hops:
        copy.wait_recv()
    sums = []
    for level in range(1, levels):
        total = None
        for i, (at_level, _) in enumerate(targets):
            if at_level == level:
                part = recv_b[i].astype(F32)
                total = part if total is None else total + part
        sums.append(jnp.concatenate([total[0], total[1]], axis=0))
    if sums:
        apply(jnp.concatenate(sums, axis=1), rank, levels * rank)

    for pair in gathers:
        for copy in pair:
            copy.wait_send()
    swap.wait_send()
    for copy in hops:
        copy.wait_send()


def on_device(coords, probes, lengthscales, amplitude, landmarks, coupling):
    groups = lax.axis_size("cols")
    levels = lax.axis_size("rows").bit_length() - 1
    dims, width = coords.shape
    count, rank = probes.shape[0], coupling.shape[0]
    others = max(groups - 1, 1)
    hops = max(2 ** (levels - 1) - 1, 1)
    upper = max(levels - 1, 1)
    vmem = pl.BlockSpec(memory_space=pltpu.VMEM)
    smem = pl.BlockSpec(memory_space=pltpu.SMEM)
    wire = F32
    return pl.pallas_call(
        functools.partial(kernel, groups, levels),
        out_shape=jax.ShapeDtypeStruct((2, count, width), F32),
        in_specs=[smem, smem, vmem, vmem, vmem, vmem],
        out_specs=vmem,
        scratch_shapes=[
            pltpu.VMEM((count, width), BF16),
            pltpu.VMEM((others, dims, width), jnp.int32),
            pltpu.VMEM((others, count, width), BF16),
            pltpu.VMEM((width + levels * rank, LANES), BF16),
            pltpu.VMEM((4, levels, rank, width), BF16),
            pltpu.VMEM((4, levels * rank, width), BF16),
            pltpu.VMEM((levels, 2, count, rank), F32),
            pltpu.VMEM((levels, 2, count, rank), wire),
            pltpu.VMEM((levels, 2, count, rank), wire),
            pltpu.VMEM((upper, 2, count, rank), wire),
            pltpu.VMEM((hops, 2, count, rank), wire),
            pltpu.SemaphoreType.DMA((others, 2)),
            pltpu.SemaphoreType.DMA((others, 2)),
            pltpu.SemaphoreType.DMA,
            pltpu.SemaphoreType.DMA,
            pltpu.SemaphoreType.DMA((hops,)),
            pltpu.SemaphoreType.DMA((hops,)),
        ],
        compiler_params=pltpu.CompilerParams(collective_id=0, has_side_effects=True),
    )(lengthscales, amplitude, coords, probes, landmarks, coupling)


def solution(mesh):
    in_specs = (P(None, ("rows", "cols")), P(None, ("rows", "cols")), P(), P(), P(), P())
    out_specs = P(None, None, ("rows", "cols"))
    return jax.shard_map(
        on_device, mesh=mesh, in_specs=in_specs, out_specs=out_specs, check_vma=False
    )
```

```python
import functools
import math

import jax
import jax.numpy as jnp
from jax import lax
from jax.experimental import pallas as pl
from jax.experimental.pallas import tpu as pltpu
from jax.sharding import PartitionSpec as P

F32 = jnp.float32
BF16 = jnp.bfloat16
HALF_LOG2E = 0.5 / math.log(2.0)
UNIT = HALF_LOG2E / 4096.0**2
MESH = pl.DeviceIdType.MESH
LANES = 128


def toggled(index, mask):
    bit = 1
    while bit <= mask:
        if mask & bit:
            index = index + bit - 2 * bit * ((index // bit) % 2)
        bit *= 2
    return index


def halves(x):
    high = x.astype(BF16)
    return high, (x - high.astype(F32)).astype(BF16)


def thirds(x):
    first = x.astype(BF16).astype(F32)
    rest = x - first
    second = rest.astype(BF16).astype(F32)
    return first, second, rest - second


def rows_of(pieces, shape):
    at = lax.broadcasted_iota(jnp.int32, shape, 0)
    out = jnp.zeros(shape, F32)
    for i, piece in enumerate(pieces):
        out = jnp.where(at == i, piece, out)
    return out


def padded(groups):
    n = groups[0].shape[1]
    rest = LANES - sum(g.shape[0] for g in groups)
    return jnp.concatenate(groups + [jnp.zeros((rest, n), F32)], axis=0)


def dot(a, b):
    return jnp.dot(a, b, preferred_element_type=F32)


def dot_t(a, b):
    return lax.dot_general(a, b, (((1,), (1,)), ((), ())), preferred_element_type=F32)


def kernel(
    groups, levels,
    scale_ref, amp_ref, coords_ref, probes_ref, land_ref, coup_ref, out_ref,
    half, cbuf, pbuf, lhs, near, fac, grown, proj, send_a, recv_a, send_b, recv_b,
    gs_sem, gr_sem, as_sem, ar_sem, bs_sem, br_sem,
):
    row, col = lax.axis_index("rows"), lax.axis_index("cols")
    width = coords_ref.shape[1]
    probes = probes_ref.shape[0]
    rank = coup_ref.shape[0]

    targets = []
    for level in range(1, levels):
        for m in range(2 ** (level - 1)):
            targets.append((level, (1 << level) ^ (2 * m)))
    peers = [(row, toggled(col, k)) for k in range(1, groups)]
    peers.append((toggled(row, 1), col))
    peers += [(toggled(row, mask), col) for _, mask in targets]

    barrier = pltpu.get_barrier_semaphore()
    for peer in peers:
        pl.semaphore_signal(barrier, inc=1, device_id=peer, device_id_type=MESH)
    half[...] = probes_ref[...].astype(BF16)
    pl.semaphore_wait(barrier, len(peers))

    gathers = [[], []]
    for i, (src, dst) in enumerate(((coords_ref, cbuf), (half, pbuf))):
        for k in range(1, groups):
            copy = pltpu.make_async_remote_copy(
                src_ref=src, dst_ref=dst.at[k - 1], send_sem=gs_sem.at[k - 1, i], recv_sem=gr_sem.at[k - 1, i],
                device_id=(row, toggled(col, k)), device_id_type=MESH,
            )
            copy.start()
            gathers[i].append(copy)

    at = lax.broadcasted_iota(jnp.int32, (8, LANES), 0)
    scales = jnp.ones((8, LANES), F32)
    for d in range(8):
        scales = jnp.where(at == d, scale_ref[d], scales)
    weight = (1.0 / (scales * scales))[:, :1] * UNIT
    log_amp = jnp.log(jnp.full((1, LANES), amp_ref[0], F32)) * (1.0 / math.log(2.0))
    log_amp = log_amp[:, :1]
    offset = log_amp * (1.0 / HALF_LOG2E)
    slant = 1.0 / HALF_LOG2E

    def centred(coords):
        return (coords - 2048).astype(F32)

    own = centred(coords_ref[...])
    anchors = []
    for level in range(levels):
        depth = levels - level
        chosen = land_ref[2**depth - 2 + row // (1 << level)]
        anchors.append((chosen - 0.5) * 4096.0)
    left = jnp.concatenate([own] + anchors, axis=1)
    weighted = weight * left
    y1, y2, y3 = thirds(2.0 * weighted)
    norm = log_amp - jnp.sum(weighted * left, axis=0, keepdims=True)
    ones = jnp.ones_like(norm)
    special = rows_of(list(thirds(norm)) + [ones] * 3, left.shape)
    lhs[...] = jnp.transpose(padded([y1, y1, y2, y2, y3, y3, special])).astype(BF16)

    def features(coords):
        value = centred(coords)
        high = value.astype(BF16).astype(F32)
        low = value - high
        norm = -jnp.sum(weight * value * value, axis=0, keepdims=True)
        ones = jnp.ones_like(norm)
        special = rows_of([ones] * 3 + list(thirds(norm)), value.shape)
        return padded([high, low, high, low, high, low, special]).astype(BF16)

    def pair_of(start, feat):
        power = dot(lhs[start : start + LANES, :], feat)
        kern = jnp.exp2(power)
        return kern, kern * (offset - slant * power)

    def diagonal_pairs(k, feat):
        for j in range(width // LANES):
            kern, slope = pair_of(j * LANES, feat)
            near[k, j, :LANES, :] = kern.astype(BF16)
            near[k, j, LANES:, :] = slope.astype(BF16)

    def anchor_pairs(k, feat):
        for level in range(levels):
            kern, slope = pair_of(width + level * rank, feat)
            for i, piece in enumerate(halves(kern) + halves(slope)):
                fac[k, level, i * rank : (i + 1) * rank, :] = piece

    def diagonal(k, signs):
        for j in range(width // LANES):
            got = dot_t(signs, near[k, j])
            for i in range(2):
                part = got[:, i * LANES : (i + 1) * LANES]
                if k == 0:
                    out_ref[i, :, j * LANES : (j + 1) * LANES] = part
                else:
                    out_ref[i, :, j * LANES : (j + 1) * LANES] += part

    def project(k, signs):
        for level in range(levels - 1, -1, -1):
            got = dot_t(signs, fac[k, level])
            for i in range(2):
                part = got[:, 2 * i * rank : (2 * i + 1) * rank] + got[:, (2 * i + 1) * rank : (2 * i + 2) * rank]
                if k == 0:
                    proj[level, i] = part
                else:
                    proj[level, i] += part

    feat = features(coords_ref[...])
    anchor_pairs(0, feat)
    diagonal_pairs(0, feat)
    for k in range(1, groups):
        gathers[0][k - 1].wait_recv()
        feat = features(cbuf[k - 1])
        anchor_pairs(k, feat)
        diagonal_pairs(k, feat)

    project(0, half[...])
    diagonal(0, half[...])

    coupling = coup_ref[...]
    flipped = jnp.transpose(coupling)
    for level in range(levels):
        side = ((row // (1 << level)) % 2).astype(F32)
        core = jnp.where(jnp.full((rank, rank), side) < 0.5, flipped, coupling)
        high, low = halves(core)
        both = jnp.concatenate([high, low], axis=0)
        for i in range(2):
            got = dot(both, fac[0, level, 2 * i * rank : (2 * i + 1) * rank, :])
            rest = dot(high, fac[0, level, (2 * i + 1) * rank : (2 * i + 2) * rank, :])
            g_high, g_low = halves(got[:rank] + got[rank:] + rest)
            grown[2 * i, level * rank : (level + 1) * rank, :] = g_high
            grown[2 * i + 1, level * rank : (level + 1) * rank, :] = g_low

    for k in range(1, groups):
        gathers[1][k - 1].wait_recv()
        project(k, pbuf[k - 1])
        if k < groups - 1:
            diagonal(k, pbuf[k - 1])

    swaps = []
    for i, (low, high) in enumerate(((1, levels), (0, 1))):
        if high > low:
            send_a[low:high] = proj[low:high].astype(send_a.dtype)
            copy = pltpu.make_async_remote_copy(
                src_ref=send_a.at[low:high], dst_ref=recv_a.at[low:high],
                send_sem=as_sem.at[i], recv_sem=ar_sem.at[i],
                device_id=(toggled(row, 1), col), device_id_type=MESH,
            )
            copy.start()
            swaps.append(copy)
    if groups > 1:
        diagonal(groups - 1, pbuf[groups - 2])
    for copy in swaps[:-1]:
        copy.wait_recv()

    send_b[...] = (proj[1:] + recv_a[1:].astype(F32)).astype(send_b.dtype)
    hops = []
    for i, (level, mask) in enumerate(targets):
        copy = pltpu.make_async_remote_copy(
            src_ref=send_b.at[level - 1], dst_ref=recv_b.at[i], send_sem=bs_sem.at[i], recv_sem=br_sem.at[i],
            device_id=(toggled(row, mask), col), device_id_type=MESH,
        )
        copy.start()
        hops.append(copy)

    def apply(sums, low_row, high_row):
        high, low = halves(sums)
        both = jnp.concatenate([high, low], axis=0)
        g = [grown[i, low_row:high_row, :] for i in range(4)]
        a = dot(both, g[0])
        b = dot(high, g[1])
        c = dot(jnp.concatenate([high[:probes], low[:probes]], axis=0), g[2])
        d = dot(high[:probes], g[3])
        plain = a[: 2 * probes] + a[2 * probes :] + b
        out_ref[0] += plain[:probes]
        out_ref[1] += plain[probes:] + c[:probes] + c[probes:] + d

    swaps[-1].wait_recv()
    apply(jnp.concatenate([recv_a[0, 0], recv_a[0, 1]], axis=0).astype(F32), 0, rank)
    for copy in hops:
        copy.wait_recv()
    sums = []
    for level in range(1, levels):
        total = None
        for i, (at_level, _) in enumerate(targets):
            if at_level == level:
                part = recv_b[i].astype(F32)
                total = part if total is None else total + part
        sums.append(jnp.concatenate([total[0], total[1]], axis=0))
    if sums:
        apply(jnp.concatenate(sums, axis=1), rank, levels * rank)

    for copy in gathers[0] + gathers[1] + swaps + hops:
        copy.wait_send()


def on_device(coords, probes, lengthscales, amplitude, landmarks, coupling):
    groups = lax.axis_size("cols")
    levels = lax.axis_size("rows").bit_length() - 1
    dims, width = coords.shape
    count, rank = probes.shape[0], coupling.shape[0]
    others = max(groups - 1, 1)
    hops = max(2 ** (levels - 1) - 1, 1)
    upper = max(levels - 1, 1)
    vmem = pl.BlockSpec(memory_space=pltpu.VMEM)
    smem = pl.BlockSpec(memory_space=pltpu.SMEM)
    wire = F32
    return pl.pallas_call(
        functools.partial(kernel, groups, levels),
        out_shape=pltpu.VMEM((2, count, width), F32),
        in_specs=[smem, smem, vmem, vmem, vmem, vmem],
        out_specs=vmem,
        scratch_shapes=[
            pltpu.VMEM((count, width), BF16),
            pltpu.VMEM((others, dims, width), jnp.int32),
            pltpu.VMEM((others, count, width), BF16),
            pltpu.VMEM((width + levels * rank, LANES), BF16),
            pltpu.VMEM((groups, width // LANES, 2 * LANES, width), BF16),
            pltpu.VMEM((groups, levels, 4 * rank, width), BF16),
            pltpu.VMEM((4, levels * rank, width), BF16),
            pltpu.VMEM((levels, 2, count, rank), F32),
            pltpu.VMEM((levels, 2, count, rank), wire),
            pltpu.VMEM((levels, 2, count, rank), wire),
            pltpu.VMEM((upper, 2, count, rank), wire),
            pltpu.VMEM((hops, 2, count, rank), wire),
            pltpu.SemaphoreType.DMA((others, 2)),
            pltpu.SemaphoreType.DMA((others, 2)),
            pltpu.SemaphoreType.DMA((2,)),
            pltpu.SemaphoreType.DMA((2,)),
            pltpu.SemaphoreType.DMA((hops,)),
            pltpu.SemaphoreType.DMA((hops,)),
        ],
        compiler_params=pltpu.CompilerParams(collective_id=0, has_side_effects=True),
    )(lengthscales, amplitude, coords, probes, landmarks, coupling)


def solution(mesh):
    in_specs = (P(None, ("rows", "cols")), P(None, ("rows", "cols")), P(), P(), P(), P())
    out_specs = P(None, None, ("rows", "cols"))
    return jax.shard_map(
        on_device, mesh=mesh, in_specs=in_specs, out_specs=out_specs, check_vma=False
    )
```

```python
import functools
import math

import jax
import jax.numpy as jnp
from jax import lax
from jax.experimental import pallas as pl
from jax.experimental.pallas import tpu as pltpu
from jax.sharding import PartitionSpec as P

F32 = jnp.float32
BF16 = jnp.bfloat16
HALF_LOG2E = 0.5 / math.log(2.0)
UNIT = HALF_LOG2E / 4096.0**2
MESH = pl.DeviceIdType.MESH
LANES = 128


def toggled(index, mask):
    bit = 1
    while bit <= mask:
        if mask & bit:
            index = index + bit - 2 * bit * ((index // bit) % 2)
        bit *= 2
    return index


def halves(x):
    high = x.astype(BF16)
    return high, (x - high.astype(F32)).astype(BF16)


def thirds(x):
    first = x.astype(BF16).astype(F32)
    rest = x - first
    second = rest.astype(BF16).astype(F32)
    return first, second, rest - second


def rows_of(pieces, shape):
    at = lax.broadcasted_iota(jnp.int32, shape, 0)
    out = jnp.zeros(shape, F32)
    for i, piece in enumerate(pieces):
        out = jnp.where(at == i, piece, out)
    return out


def padded(groups):
    n = groups[0].shape[1]
    rest = LANES - sum(g.shape[0] for g in groups)
    return jnp.concatenate(groups + [jnp.zeros((rest, n), F32)], axis=0)


def dot(a, b):
    return jnp.dot(a, b, preferred_element_type=F32)


def dot_t(a, b):
    return lax.dot_general(a, b, (((1,), (1,)), ((), ())), preferred_element_type=F32)


def kernel(
    groups, levels,
    scale_hbm, amp_hbm, coords_hbm, probes_hbm, land_hbm, coup_hbm, out_ref,
    scale_ref, amp_ref, coords_ref, probes_ref, land_ref, coup_ref, in_sem, half, cbuf, pbuf, lhs, near, fac, grown, proj, send_a, recv_a, send_b, recv_b,
    gs_sem, gr_sem, as_sem, ar_sem, bs_sem, br_sem,
):
    row, col = lax.axis_index("rows"), lax.axis_index("cols")
    width = coords_ref.shape[1]
    probes = probes_ref.shape[0]
    rank = coup_ref.shape[0]

    targets = []
    for level in range(1, levels):
        for m in range(2 ** (level - 1)):
            targets.append((level, (1 << level) ^ (2 * m)))
    peers = [(row, toggled(col, k)) for k in range(1, groups)]
    peers.append((toggled(row, 1), col))
    peers += [(toggled(row, mask), col) for _, mask in targets]

    barrier = pltpu.get_barrier_semaphore()
    for peer in peers:
        pl.semaphore_signal(barrier, inc=1, device_id=peer, device_id_type=MESH)
    loads = [
        pltpu.make_async_copy(src, dst, in_sem.at[i])
        for i, (src, dst) in enumerate((
            (probes_hbm, probes_ref), (coords_hbm, coords_ref), (scale_hbm, scale_ref),
            (amp_hbm, amp_ref), (land_hbm, land_ref), (coup_hbm, coup_ref),
        ))
    ]
    for load in loads:
        load.start()
    loads[1].wait()
    loads[0].wait()
    half[...] = probes_ref[...].astype(BF16)
    pl.semaphore_wait(barrier, len(peers))

    gathers = {}
    for part, (src, dst) in enumerate(((coords_ref, cbuf), (half, pbuf))):
        for k in range(1, groups):
            gathers[k, part] = pltpu.make_async_remote_copy(
                src_ref=src, dst_ref=dst.at[k - 1], send_sem=gs_sem.at[k - 1, part], recv_sem=gr_sem.at[k - 1, part],
                device_id=(row, toggled(col, k)), device_id_type=MESH,
            )
            gathers[k, part].start()

    for load in loads[2:]:
        load.wait()

    at = lax.broadcasted_iota(jnp.int32, (8, LANES), 0)
    scales = jnp.ones((8, LANES), F32)
    for d in range(8):
        scales = jnp.where(at == d, scale_ref[d], scales)
    weight = (1.0 / (scales * scales))[:, :1] * UNIT
    log_amp = jnp.log(jnp.full((1, LANES), amp_ref[0], F32)) * (1.0 / math.log(2.0))
    log_amp = log_amp[:, :1]
    offset = log_amp * (1.0 / HALF_LOG2E)
    slant = 1.0 / HALF_LOG2E

    def centred(coords):
        return (coords - 2048).astype(F32)

    own = centred(coords_ref[...])
    anchors = []
    for level in range(levels):
        depth = levels - level
        chosen = land_ref[2**depth - 2 + row // (1 << level)]
        anchors.append((chosen - 0.5) * 4096.0)
    left = jnp.concatenate([own] + anchors, axis=1)
    weighted = weight * left
    y1, y2, y3 = thirds(2.0 * weighted)
    norm = log_amp - jnp.sum(weighted * left, axis=0, keepdims=True)
    ones = jnp.ones_like(norm)
    special = rows_of(list(thirds(norm)) + [ones] * 3, left.shape)
    lhs[...] = jnp.transpose(padded([y1, y1, y2, y2, y3, y3, special])).astype(BF16)

    def features(coords):
        value = centred(coords)
        high = value.astype(BF16).astype(F32)
        low = value - high
        norm = -jnp.sum(weight * value * value, axis=0, keepdims=True)
        ones = jnp.ones_like(norm)
        special = rows_of([ones] * 3 + list(thirds(norm)), value.shape)
        return padded([high, low, high, low, high, low, special]).astype(BF16)

    def pair_of(start, feat):
        power = dot(lhs[start : start + LANES, :], feat)
        kern = jnp.exp2(power)
        return kern, kern * (offset - slant * power)

    def diagonal_pairs(k, feat):
        for j in range(width // LANES):
            kern, slope = pair_of(j * LANES, feat)
            near[k, j, :LANES, :] = kern.astype(BF16)
            near[k, j, LANES:, :] = slope.astype(BF16)

    def anchor_pairs(k, feat):
        for level in range(levels):
            kern, slope = pair_of(width + level * rank, feat)
            for i, piece in enumerate(halves(kern) + halves(slope)):
                fac[k, level, i * rank : (i + 1) * rank, :] = piece

    def diagonal(k, signs):
        for j in range(width // LANES):
            got = dot_t(signs, near[k, j])
            for i in range(2):
                part = got[:, i * LANES : (i + 1) * LANES]
                if k == 0:
                    out_ref[i, :, j * LANES : (j + 1) * LANES] = part
                else:
                    out_ref[i, :, j * LANES : (j + 1) * LANES] += part

    def project(k, signs):
        for level in range(levels - 1, -1, -1):
            got = dot_t(signs, fac[k, level])
            for i in range(2):
                part = got[:, 2 * i * rank : (2 * i + 1) * rank] + got[:, (2 * i + 1) * rank : (2 * i + 2) * rank]
                if k == 0:
                    proj[level, i] = part
                else:
                    proj[level, i] += part

    feat = features(coords_ref[...])
    anchor_pairs(0, feat)
    diagonal_pairs(0, feat)
    for k in range(1, groups):
        gathers[k, 0].wait_recv()
        feat = features(cbuf[k - 1])
        anchor_pairs(k, feat)
        diagonal_pairs(k, feat)

    project(0, half[...])
    diagonal(0, half[...])

    coupling = coup_ref[...]
    flipped = jnp.transpose(coupling)
    for level in range(levels):
        side = ((row // (1 << level)) % 2).astype(F32)
        core = jnp.where(jnp.full((rank, rank), side) < 0.5, flipped, coupling)
        high, low = halves(core)
        both = jnp.concatenate([high, low], axis=0)
        for i in range(2):
            got = dot(both, fac[0, level, 2 * i * rank : (2 * i + 1) * rank, :])
            rest = dot(high, fac[0, level, (2 * i + 1) * rank : (2 * i + 2) * rank, :])
            g_high, g_low = halves(got[:rank] + got[rank:] + rest)
            grown[2 * i, level * rank : (level + 1) * rank, :] = g_high
            grown[2 * i + 1, level * rank : (level + 1) * rank, :] = g_low

    for k in range(1, groups):
        gathers[k, 1].wait_recv()
        project(k, pbuf[k - 1])
        if k < groups - 1:
            diagonal(k, pbuf[k - 1])

    swaps = []
    for i, (low, high) in enumerate(((1, levels), (0, 1))):
        if high > low:
            send_a[low:high] = proj[low:high].astype(send_a.dtype)
            copy = pltpu.make_async_remote_copy(
                src_ref=send_a.at[low:high], dst_ref=recv_a.at[low:high],
                send_sem=as_sem.at[i], recv_sem=ar_sem.at[i],
                device_id=(toggled(row, 1), col), device_id_type=MESH,
            )
            copy.start()
            swaps.append(copy)
    if groups > 1:
        diagonal(groups - 1, pbuf[groups - 2])
    for copy in swaps[:-1]:
        copy.wait_recv()

    send_b[...] = (proj[1:] + recv_a[1:].astype(F32)).astype(send_b.dtype)
    hops = []
    for i, (level, mask) in enumerate(targets):
        copy = pltpu.make_async_remote_copy(
            src_ref=send_b.at[level - 1], dst_ref=recv_b.at[i], send_sem=bs_sem.at[i], recv_sem=br_sem.at[i],
            device_id=(toggled(row, mask), col), device_id_type=MESH,
        )
        copy.start()
        hops.append(copy)

    def apply(sums, low_row, high_row):
        high, low = halves(sums)
        both = jnp.concatenate([high, low], axis=0)
        g = [grown[i, low_row:high_row, :] for i in range(4)]
        a = dot(both, g[0])
        b = dot(high, g[1])
        c = dot(jnp.concatenate([high[:probes], low[:probes]], axis=0), g[2])
        d = dot(high[:probes], g[3])
        plain = a[: 2 * probes] + a[2 * probes :] + b
        out_ref[0] += plain[:probes]
        out_ref[1] += plain[probes:] + c[:probes] + c[probes:] + d

    swaps[-1].wait_recv()
    apply(jnp.concatenate([recv_a[0, 0], recv_a[0, 1]], axis=0).astype(F32), 0, rank)
    for copy in hops:
        copy.wait_recv()
    sums = []
    for level in range(1, levels):
        total = None
        for i, (at_level, _) in enumerate(targets):
            if at_level == level:
                part = recv_b[i].astype(F32)
                total = part if total is None else total + part
        sums.append(jnp.concatenate([total[0], total[1]], axis=0))
    if sums:
        apply(jnp.concatenate(sums, axis=1), rank, levels * rank)

    for copy in list(gathers.values()) + swaps + hops:
        copy.wait_send()


def on_device(coords, probes, lengthscales, amplitude, landmarks, coupling):
    groups = lax.axis_size("cols")
    levels = lax.axis_size("rows").bit_length() - 1
    dims, width = coords.shape
    count, rank = probes.shape[0], coupling.shape[0]
    others = max(groups - 1, 1)
    hops = max(2 ** (levels - 1) - 1, 1)
    upper = max(levels - 1, 1)
    vmem = pl.BlockSpec(memory_space=pltpu.VMEM)
    anywhere = pl.BlockSpec(memory_space=pl.ANY)
    return pl.pallas_call(
        functools.partial(kernel, groups, levels),
        out_shape=pltpu.VMEM((2, count, width), F32),
        in_specs=[anywhere] * 6,
        out_specs=vmem,
        scratch_shapes=[
            pltpu.SMEM(lengthscales.shape, F32),
            pltpu.SMEM(amplitude.shape, F32),
            pltpu.VMEM(coords.shape, jnp.int32),
            pltpu.VMEM(probes.shape, F32),
            pltpu.VMEM(landmarks.shape, F32),
            pltpu.VMEM(coupling.shape, F32),
            pltpu.SemaphoreType.DMA((6,)),
            pltpu.VMEM((count, width), BF16),
            pltpu.VMEM((others, dims, width), jnp.int32),
            pltpu.VMEM((others, count, width), BF16),
            pltpu.VMEM((width + levels * rank, LANES), BF16),
            pltpu.VMEM((groups, width // LANES, 2 * LANES, width), BF16),
            pltpu.VMEM((groups, levels, 4 * rank, width), BF16),
            pltpu.VMEM((4, levels * rank, width), BF16),
            pltpu.VMEM((levels, 2, count, rank), F32),
            pltpu.VMEM((levels, 2, count, rank), F32),
            pltpu.VMEM((levels, 2, count, rank), F32),
            pltpu.VMEM((upper, 2, count, rank), BF16),
            pltpu.VMEM((hops, 2, count, rank), BF16),
            pltpu.SemaphoreType.DMA((others, 2)),
            pltpu.SemaphoreType.DMA((others, 2)),
            pltpu.SemaphoreType.DMA((2,)),
            pltpu.SemaphoreType.DMA((2,)),
            pltpu.SemaphoreType.DMA((hops,)),
            pltpu.SemaphoreType.DMA((hops,)),
        ],
        compiler_params=pltpu.CompilerParams(collective_id=0, has_side_effects=True),
    )(lengthscales, amplitude, coords, probes, landmarks, coupling)


def solution(mesh):
    in_specs = (P(None, ("rows", "cols")), P(None, ("rows", "cols")), P(), P(), P(), P())
    out_specs = P(None, None, ("rows", "cols"))
    return jax.shard_map(
        on_device, mesh=mesh, in_specs=in_specs, out_specs=out_specs, check_vma=False
    )
```

```python
import functools
import math

import jax
import jax.numpy as jnp
from jax import lax
from jax.experimental import pallas as pl
from jax.experimental.pallas import tpu as pltpu
from jax.sharding import PartitionSpec as P

F32 = jnp.float32
BF16 = jnp.bfloat16
HALF_LOG2E = 0.5 / math.log(2.0)
UNIT = HALF_LOG2E / 4096.0**2
MESH = pl.DeviceIdType.MESH
LANES = 128


def toggled(index, mask):
    bit = 1
    while bit <= mask:
        if mask & bit:
            index = index + bit - 2 * bit * ((index // bit) % 2)
        bit *= 2
    return index


def halves(x):
    high = x.astype(BF16)
    return high, (x - high.astype(F32)).astype(BF16)


def thirds(x):
    first = x.astype(BF16).astype(F32)
    rest = x - first
    second = rest.astype(BF16).astype(F32)
    return first, second, rest - second


def rows_of(pieces, shape):
    at = lax.broadcasted_iota(jnp.int32, shape, 0)
    out = jnp.zeros(shape, F32)
    for i, piece in enumerate(pieces):
        out = jnp.where(at == i, piece, out)
    return out


def padded(groups):
    n = groups[0].shape[1]
    rest = LANES - sum(g.shape[0] for g in groups)
    return jnp.concatenate(groups + [jnp.zeros((rest, n), F32)], axis=0)


def dot(a, b):
    return jnp.dot(a, b, preferred_element_type=F32)


def dot_t(a, b):
    return lax.dot_general(a, b, (((1,), (1,)), ((), ())), preferred_element_type=F32)


def kernel(
    groups, levels,
    scale_hbm, amp_hbm, coords_hbm, probes_hbm, land_hbm, coup_hbm, out_ref,
    scale_ref, amp_ref, coords_ref, probes_ref, land_ref, coup_ref, in_sem, half, cbuf, pbuf, lhs, near, fac, grown, proj, send_a, recv_a, send_b, recv_b,
    gs_sem, gr_sem, as_sem, ar_sem, bs_sem, br_sem,
):
    row, col = lax.axis_index("rows"), lax.axis_index("cols")
    width = coords_ref.shape[1]
    probes = probes_ref.shape[0]
    rank = coup_ref.shape[0]

    targets = []
    for level in range(1, levels):
        for m in range(2**level):
            targets.append((level, (1 << level) ^ m))
    peers = [(row, toggled(col, k)) for k in range(1, groups)]
    peers.append((toggled(row, 1), col))
    peers += [(toggled(row, mask), col) for _, mask in targets]

    barrier = pltpu.get_barrier_semaphore()
    for peer in peers:
        pl.semaphore_signal(barrier, inc=1, device_id=peer, device_id_type=MESH)
    loads = [
        pltpu.make_async_copy(src, dst, in_sem.at[i])
        for i, (src, dst) in enumerate((
            (probes_hbm, probes_ref), (coords_hbm, coords_ref), (scale_hbm, scale_ref),
            (amp_hbm, amp_ref), (land_hbm, land_ref), (coup_hbm, coup_ref),
        ))
    ]
    for load in loads:
        load.start()
    loads[1].wait()
    loads[0].wait()
    half[...] = probes_ref[...].astype(BF16)
    pl.semaphore_wait(barrier, len(peers))

    gathers = {}
    for part, (src, dst) in enumerate(((coords_ref, cbuf), (half, pbuf))):
        for k in range(1, groups):
            gathers[k, part] = pltpu.make_async_remote_copy(
                src_ref=src, dst_ref=dst.at[k - 1], send_sem=gs_sem.at[k - 1, part], recv_sem=gr_sem.at[k - 1, part],
                device_id=(row, toggled(col, k)), device_id_type=MESH,
            )
            gathers[k, part].start()

    for load in loads[2:]:
        load.wait()

    at = lax.broadcasted_iota(jnp.int32, (8, LANES), 0)
    scales = jnp.ones((8, LANES), F32)
    for d in range(8):
        scales = jnp.where(at == d, scale_ref[d], scales)
    weight = (1.0 / (scales * scales))[:, :1] * UNIT
    log_amp = jnp.log(jnp.full((1, LANES), amp_ref[0], F32)) * (1.0 / math.log(2.0))
    log_amp = log_amp[:, :1]
    offset = log_amp * (1.0 / HALF_LOG2E)
    slant = 1.0 / HALF_LOG2E

    def centred(coords):
        return (coords - 2048).astype(F32)

    own = centred(coords_ref[...])
    anchors = []
    for level in range(levels):
        depth = levels - level
        chosen = land_ref[2**depth - 2 + row // (1 << level)]
        anchors.append((chosen - 0.5) * 4096.0)
    left = jnp.concatenate([own] + anchors, axis=1)
    weighted = weight * left
    y1, y2, y3 = thirds(2.0 * weighted)
    norm = log_amp - jnp.sum(weighted * left, axis=0, keepdims=True)
    ones = jnp.ones_like(norm)
    special = rows_of(list(thirds(norm)) + [ones] * 3, left.shape)
    lhs[...] = jnp.transpose(padded([y1, y1, y2, y2, y3, y3, special])).astype(BF16)

    def features(coords):
        value = centred(coords)
        high = value.astype(BF16).astype(F32)
        low = value - high
        norm = -jnp.sum(weight * value * value, axis=0, keepdims=True)
        ones = jnp.ones_like(norm)
        special = rows_of([ones] * 3 + list(thirds(norm)), value.shape)
        return padded([high, low, high, low, high, low, special]).astype(BF16)

    def pair_of(start, feat):
        power = dot(lhs[start : start + LANES, :], feat)
        kern = jnp.exp2(power)
        return kern, kern * (offset - slant * power)

    def diagonal_pairs(k, feat):
        for j in range(width // LANES):
            kern, slope = pair_of(j * LANES, feat)
            near[k, j, :LANES, :] = kern.astype(BF16)
            near[k, j, LANES:, :] = slope.astype(BF16)

    def anchor_pairs(k, feat):
        for level in range(levels):
            kern, slope = pair_of(width + level * rank, feat)
            for i, piece in enumerate(halves(kern) + halves(slope)):
                fac[k, level, i * rank : (i + 1) * rank, :] = piece

    def diagonal(k, signs):
        for j in range(width // LANES):
            got = dot_t(signs, near[k, j])
            for i in range(2):
                part = got[:, i * LANES : (i + 1) * LANES]
                if k == 0:
                    out_ref[i, :, j * LANES : (j + 1) * LANES] = part
                else:
                    out_ref[i, :, j * LANES : (j + 1) * LANES] += part

    def project(k, signs):
        for level in range(levels - 1, -1, -1):
            got = dot_t(signs, fac[k, level])
            for i in range(2):
                part = got[:, 2 * i * rank : (2 * i + 1) * rank] + got[:, (2 * i + 1) * rank : (2 * i + 2) * rank]
                if k == 0:
                    proj[level, i] = part
                else:
                    proj[level, i] += part

    feat = features(coords_ref[...])
    anchor_pairs(0, feat)
    diagonal_pairs(0, feat)
    for k in range(1, groups):
        gathers[k, 0].wait_recv()
        feat = features(cbuf[k - 1])
        anchor_pairs(k, feat)
        diagonal_pairs(k, feat)

    project(0, half[...])
    diagonal(0, half[...])

    coupling = coup_ref[...]
    flipped = jnp.transpose(coupling)
    for level in range(levels):
        side = ((row // (1 << level)) % 2).astype(F32)
        core = jnp.where(jnp.full((rank, rank), side) < 0.5, flipped, coupling)
        high, low = halves(core)
        both = jnp.concatenate([high, low], axis=0)
        for i in range(2):
            got = dot(both, fac[0, level, 2 * i * rank : (2 * i + 1) * rank, :])
            rest = dot(high, fac[0, level, (2 * i + 1) * rank : (2 * i + 2) * rank, :])
            g_high, g_low = halves(got[:rank] + got[rank:] + rest)
            grown[2 * i, level * rank : (level + 1) * rank, :] = g_high
            grown[2 * i + 1, level * rank : (level + 1) * rank, :] = g_low

    for k in range(1, groups):
        gathers[k, 1].wait_recv()
        project(k, pbuf[k - 1])
        if k < groups - 1:
            diagonal(k, pbuf[k - 1])

    send_b[...] = proj[1:].astype(send_b.dtype)
    hops = []
    for i, (level, mask) in reversed(list(enumerate(targets))):
        copy = pltpu.make_async_remote_copy(
            src_ref=send_b.at[level - 1], dst_ref=recv_b.at[i], send_sem=bs_sem.at[i], recv_sem=br_sem.at[i],
            device_id=(toggled(row, mask), col), device_id_type=MESH,
        )
        copy.start()
        hops.append(copy)
    send_a[...] = proj[:1]
    swap = pltpu.make_async_remote_copy(
        src_ref=send_a, dst_ref=recv_a, send_sem=as_sem, recv_sem=ar_sem,
        device_id=(toggled(row, 1), col), device_id_type=MESH,
    )
    swap.start()
    if groups > 1:
        diagonal(groups - 1, pbuf[groups - 2])

    def apply(sums, low_row, high_row):
        high, low = halves(sums)
        both = jnp.concatenate([high, low], axis=0)
        g = [grown[i, low_row:high_row, :] for i in range(4)]
        a = dot(both, g[0])
        b = dot(high, g[1])
        c = dot(jnp.concatenate([high[:probes], low[:probes]], axis=0), g[2])
        d = dot(high[:probes], g[3])
        plain = a[: 2 * probes] + a[2 * probes :] + b
        out_ref[0] += plain[:probes]
        out_ref[1] += plain[probes:] + c[:probes] + c[probes:] + d

    swap.wait_recv()
    apply(jnp.concatenate([recv_a[0, 0], recv_a[0, 1]], axis=0).astype(F32), 0, rank)
    for copy in hops:
        copy.wait_recv()
    sums = []
    for level in range(1, levels):
        total = None
        for i, (at_level, _) in enumerate(targets):
            if at_level == level:
                part = recv_b[i].astype(F32)
                total = part if total is None else total + part
        sums.append(jnp.concatenate([total[0], total[1]], axis=0))
    if sums:
        apply(jnp.concatenate(sums, axis=1), rank, levels * rank)

    for copy in list(gathers.values()) + [swap] + hops:
        copy.wait_send()


def on_device(coords, probes, lengthscales, amplitude, landmarks, coupling):
    groups = lax.axis_size("cols")
    levels = lax.axis_size("rows").bit_length() - 1
    dims, width = coords.shape
    count, rank = probes.shape[0], coupling.shape[0]
    others = max(groups - 1, 1)
    hops = max(2**levels - 2, 1)
    upper = max(levels - 1, 1)
    vmem = pl.BlockSpec(memory_space=pltpu.VMEM)
    anywhere = pl.BlockSpec(memory_space=pltpu.HBM)
    return pl.pallas_call(
        functools.partial(kernel, groups, levels),
        out_shape=pltpu.VMEM((2, count, width), F32),
        in_specs=[anywhere] * 6,
        out_specs=vmem,
        scratch_shapes=[
            pltpu.SMEM(lengthscales.shape, F32),
            pltpu.SMEM(amplitude.shape, F32),
            pltpu.VMEM(coords.shape, jnp.int32),
            pltpu.VMEM(probes.shape, F32),
            pltpu.VMEM(landmarks.shape, F32),
            pltpu.VMEM(coupling.shape, F32),
            pltpu.SemaphoreType.DMA((6,)),
            pltpu.VMEM((count, width), BF16),
            pltpu.VMEM((others, dims, width), jnp.int32),
            pltpu.VMEM((others, count, width), BF16),
            pltpu.VMEM((width + levels * rank, LANES), BF16),
            pltpu.VMEM((groups, width // LANES, 2 * LANES, width), BF16),
            pltpu.VMEM((groups, levels, 4 * rank, width), BF16),
            pltpu.VMEM((4, levels * rank, width), BF16),
            pltpu.VMEM((levels, 2, count, rank), F32),
            pltpu.VMEM((1, 2, count, rank), F32),
            pltpu.VMEM((1, 2, count, rank), F32),
            pltpu.VMEM((upper, 2, count, rank), BF16),
            pltpu.VMEM((hops, 2, count, rank), BF16),
            pltpu.SemaphoreType.DMA((others, 2)),
            pltpu.SemaphoreType.DMA((others, 2)),
            pltpu.SemaphoreType.DMA,
            pltpu.SemaphoreType.DMA,
            pltpu.SemaphoreType.DMA((hops,)),
            pltpu.SemaphoreType.DMA((hops,)),
        ],
        compiler_params=pltpu.CompilerParams(collective_id=0, has_side_effects=True),
    )(lengthscales, amplitude, coords, probes, landmarks, coupling)


def solution(mesh):
    in_specs = (P(None, ("rows", "cols")), P(None, ("rows", "cols")), P(), P(), P(), P())
    out_specs = P(None, None, ("rows", "cols"))
    return jax.shard_map(
        on_device, mesh=mesh, in_specs=in_specs, out_specs=out_specs, check_vma=False
    )
```
